256 devices in a mesh: depth: 32 (over x, y, z_lo), kslab: 8 (over z_hi, core).
Axes of the slice: x: 4, y: 4, z: 8 (z_hi: 4, z_lo: 2; z = z_hi * 2 + z_lo), core: 2. Of those that a mesh axis runs over, the one named last changes fastest.
Arguments:
- spectra: bfloat16 [32, 2, 512, 1024], P('depth', None, 'kslab'), may hold values from -6 to 6
- green: bfloat16 [32, 32, 2, 512, 1024], P('depth', None, None, 'kslab'), may hold values from -1 to 1, as said below
- contrast: float32 [32, 512, 1024], P('depth', None, 'kslab'), may hold values from 0.3 to 3
Outputs:
- applied: bfloat16 [32, 2, 512, 1024], P('depth', None, None, 'kslab')
The draws below stay inside these ranges and needn't reach their ends.
Inputs may be any that keep to these rules, and one draw needn't show every extreme that they name: green[t, s] equals green[s, t] for every pair of layers (reciprocity).
All inputs are finite; a program needn't handle non-finite values.
Results may differ from the reference program's by a relative error of at most 0.007.
Values may be sent and summed in bfloat16 or wider, within the bound.
A program may use at most 128 MiB of HBM per device.

```python
import math
import jax
import jax.numpy as jnp
from jax import lax

NX = 512
NY = 1024
LAYERS = 32


def draw_green(key, part):
    layer_ids = jnp.arange(LAYERS, dtype=jnp.int32)

    def one_pair(target, source):
        lower_layer = jnp.minimum(target, source)
        upper_layer = jnp.maximum(target, source)
        pair_key = jax.random.fold_in(key, lower_layer * LAYERS + upper_layer)
        entries = jax.random.normal(pair_key, (2, NX, NY), jnp.float32)
        return jnp.clip(entries / math.sqrt(LAYERS), -1.0, 1.0).astype(jnp.bfloat16)

    def one_row(target):
        return jax.vmap(lambda source: one_pair(target, source))(layer_ids)
    return lax.map(one_row, layer_ids)


def level_of(key, dims, cuts, low, largest):
    loudness = 1.0
    for axis_at, parts in cuts:
        steps = jax.random.uniform(jax.random.fold_in(jax.random.fold_in(key, 6), axis_at), (parts,), jnp.float32, low / len(cuts), largest / len(cuts))
        loudness = loudness * jnp.repeat(jnp.exp(steps), dims[axis_at] // parts).reshape((-1,) + (1,) * (len(dims) - 1 - axis_at))
    return loudness


def bell_draw(rng, shape, spread, most, pieces=(), kind=jnp.bfloat16):
    result = jax.random.normal(rng, shape, jnp.float32) * spread
    if len(pieces) > 0:
        result = level_of(rng, shape, pieces, -0.22, 0.18) * result
    return jnp.clip(result, min=-most, max=most).astype(kind)


def setup_inputs(seed: int = 0) -> dict:
    keys = jax.random.split(jax.random.key(seed), 4)
    return {
        "spectra": bell_draw(keys[0], (LAYERS, 2, NX, NY), 1.0, 6.0, ((0, 32), (2, 8))),
        "green": draw_green(jax.random.fold_in(keys[3], 71), 0),
        "contrast": jnp.clip(jnp.exp(math.log(3.0) - 2.3025851 * jax.random.uniform(keys[2], (LAYERS, NX, NY), jnp.float32) ** level_of(keys[2], (LAYERS, NX, NY), ((0, 32), (2, 8)), -0.2, 0.2)), 0.3, 3.0),
    }


def fourier_tables(length):
    indices = jnp.arange(length, dtype=jnp.int32)
    products = indices[:, None] * indices[None, :] % length
    angles = products.astype(jnp.float32) * (2.0 * math.pi / length)
    factor = 1.0 / math.sqrt(length)
    return ((jnp.cos(angles) * factor).astype(jnp.bfloat16), (jnp.sin(angles) * factor).astype(jnp.bfloat16))

def reference(spectra, green, contrast):
    cos_y, sin_y = fourier_tables(NY)
    table_y = jnp.concatenate([cos_y, sin_y], axis=1)
    cos_x, sin_x = fourier_tables(NX)
    table_x = jnp.concatenate([cos_x, sin_x], axis=0)
    sources = spectra.astype(jnp.float32)

    def one_target(target):
        coeffs = green[target].astype(jnp.float32)
        real_part = lax.optimization_barrier(jnp.sum(coeffs[:, 0] * sources[:, 0] - coeffs[:, 1] * sources[:, 1], axis=0))
        imag_part = lax.optimization_barrier(jnp.sum(coeffs[:, 0] * sources[:, 1] + coeffs[:, 1] * sources[:, 0], axis=0))
        summed = jnp.stack([real_part, imag_part]).astype(jnp.bfloat16)
        section_one = jnp.dot(summed.reshape(2 * NX, NY), table_y, preferred_element_type=jnp.float32)
        halfway = jnp.stack([section_one[:NX, :NY] - section_one[NX:, NY:], section_one[:NX, NY:] + section_one[NX:, :NY]]).astype(jnp.bfloat16)
        from_real = jnp.dot(table_x, halfway[0], preferred_element_type=jnp.float32)
        from_imag = jnp.dot(table_x, halfway[1], preferred_element_type=jnp.float32)
        field_out = jnp.stack([from_real[:NX] - from_imag[NX:], from_real[NX:] + from_imag[:NX]])
        return (field_out * contrast[target][None]).astype(jnp.bfloat16)
    return lax.map(one_target, jnp.arange(LAYERS, dtype=jnp.int32))
```

```python
import functools
import math

import jax
import jax.numpy as jnp
import ml_dtypes
import numpy as np
from jax import lax
from jax.experimental import pallas as pl
from jax.experimental.pallas import tpu as pltpu
from jax.sharding import PartitionSpec as P

NX = 512
NY = 1024
LAYERS = 32
SLABS = 8
ROWS = NX // SLABS
COLS = NY // SLABS
CHUNKS = 2
R = ROWS // CHUNKS
MESH = pl.DeviceIdType.MESH


def fourier_tables(length):
    indices = np.arange(length, dtype=np.int64)
    products = indices[:, None] * indices[None, :] % length
    angles = products.astype(np.float64) * (2.0 * math.pi / length)
    factor = 1.0 / math.sqrt(length)
    return (
        (np.cos(angles) * factor).astype(np.float32).astype(ml_dtypes.bfloat16),
        (np.sin(angles) * factor).astype(np.float32).astype(ml_dtypes.bfloat16),
    )


def kernel(
    spectra, green, contrast, table_y, table_x, out,
    held, coeffs, ty, tx, con, summed, outgoing, halves,
    own_sem, load_sem, send_sem, recv_sem, swap_send, swap_recv,
):
    depth = lax.axis_index("depth")
    slab = lax.axis_index("kslab")
    at_x, at_y, at_z = depth // 8, (depth // 2) % 4, depth % 2

    def own_copy(c, p):
        return pltpu.make_async_copy(
            spectra.at[0, p, pl.ds(c * R, R)], held.at[c, p, depth], own_sem.at[c, p]
        )

    for c in range(CHUNKS):
        for p in range(2):
            own_copy(c, p).start()
    loads = [
        pltpu.make_async_copy(green.at[0], coeffs, load_sem.at[0]),
        pltpu.make_async_copy(table_y, ty, load_sem.at[1]),
        pltpu.make_async_copy(table_x, tx, load_sem.at[2]),
        pltpu.make_async_copy(contrast.at[0], con, load_sem.at[3]),
    ]
    for load in loads:
        load.start()

    def layer(p, dz, da, db):
        ca = at_x * (1 - p) + at_y * p
        cb = at_y * (1 - p) + at_x * p
        return (
            (ca + da + 4) % 4 * (8 - 6 * p)
            + (cb + db + 4) % 4 * (2 + 6 * p)
            + (at_z + dz) % 2
        )

    barrier = pltpu.get_barrier_semaphore()
    for other in (
        layer(0, 1, 0, 0), layer(0, 0, 1, 0), layer(0, 0, -1, 0),
        layer(0, 0, 0, 1), layer(0, 0, 0, -1),
    ):
        pl.semaphore_signal(
            barrier, inc=1, device_id={"depth": other}, device_id_type=MESH
        )
    for k in range(1, SLABS):
        pl.semaphore_signal(
            barrier, inc=1, device_id={"kslab": (slab + k) % SLABS}, device_id_type=MESH
        )
    pl.semaphore_wait(barrier, 5 + SLABS - 1)

    def send(c, p, block, to, half=None):
        ref = held.at[c, p, block]
        if half is not None:
            ref = held.at[c, p, block, pl.ds(half * (R // 2), R // 2)]
        pltpu.make_async_remote_copy(
            src_ref=ref, dst_ref=ref,
            send_sem=send_sem.at[c, p], recv_sem=recv_sem.at[c, p, block],
            device_id={"depth": to}, device_id_type=MESH,
        ).start()

    def arrived(c, p, block):
        ref = held.at[c, p, block]
        pltpu.make_async_remote_copy(
            src_ref=ref, dst_ref=ref,
            send_sem=send_sem.at[c, p], recv_sem=recv_sem.at[c, p, block],
            device_id={"depth": layer(0, 1, 0, 0)}, device_id_type=MESH,
        ).wait_recv()

    def along_a(c, p, block):
        send(c, p, block, layer(p, 0, 1, 0))
        send(c, p, block, layer(p, 0, -1, 0))

    def along_b(c, p, block):
        send(c, p, block, layer(p, 0, 0, 1))
        send(c, p, block, layer(p, 0, 0, -1))

    def both_parts(step):
        def body(p, carry):
            step(p)
            return carry
        lax.fori_loop(0, 2, body, 0)

    def first(c):
        def step(p):
            own_copy(c, p).wait()
            send(c, p, depth, layer(p, 1, 0, 0))
            along_a(c, p, depth)
        both_parts(step)
        both_parts(lambda p: along_b(c, p, depth))

    def partner(c):
        def step(p):
            block = layer(p, 1, 0, 0)
            arrived(c, p, block)
            along_a(c, p, block)
            along_b(c, p, block)
        both_parts(step)

    def near(c, dz):
        def step(p):
            before, after = layer(p, dz, -1, 0), layer(p, dz, 1, 0)
            arrived(c, p, before)
            send(c, p, before, layer(p, 0, 1, 0), 0)
            arrived(c, p, after)
            send(c, p, after, layer(p, 0, -1, 0), 1)
            along_b(c, p, before)
            along_b(c, p, after)
        both_parts(step)

    def far(c, dz):
        def step(p):
            block = layer(p, dz, 2, 0)
            arrived(c, p, block)
            along_b(c, p, block)
        both_parts(step)

    def relay(c, da):
        def step(p):
            def each(dz, carry):
                before, after = layer(p, dz, da, -1), layer(p, dz, da, 1)
                arrived(c, p, before)
                send(c, p, before, layer(p, 0, 0, 1), 0)
                arrived(c, p, after)
                send(c, p, after, layer(p, 0, 0, -1), 1)
                return carry
            lax.fori_loop(0, 2, each, 0)
        both_parts(step)

    def last(c):
        def step(p):
            def each(i, carry):
                arrived(c, p, layer(p, i // 4, i % 4, 2))
                return carry
            lax.fori_loop(0, 8, each, 0)
        both_parts(step)

    def contract(c):
        def column(j, carry):
            cs = pl.ds(pl.multiple_of(j * 128, 128), 128)

            def body(s, acc):
                gr = coeffs[s, 0, pl.ds(c * R, R), cs].astype(jnp.float32)
                gi = coeffs[s, 1, pl.ds(c * R, R), cs].astype(jnp.float32)
                xr = held[c, 0, s, :, cs].astype(jnp.float32)
                xi = held[c, 1, s, :, cs].astype(jnp.float32)
                return acc[0] + (gr * xr - gi * xi), acc[1] + (gr * xi + gi * xr)

            zero = jnp.zeros((R, 128), jnp.float32)
            re, im = lax.fori_loop(0, LAYERS, body, (zero, zero), unroll=4)
            summed[pl.ds(0, R), cs] = re.astype(jnp.bfloat16)
            summed[pl.ds(R, R), cs] = im.astype(jnp.bfloat16)
            return carry
        lax.fori_loop(0, NY // 128, column, 0)

    def swap(c, to):
        return pltpu.make_async_remote_copy(
            src_ref=outgoing.at[c, to], dst_ref=halves.at[slab, c],
            send_sem=swap_send.at[c, to], recv_sem=swap_recv.at[c, slab],
            device_id={"kslab": to}, device_id_type=MESH,
        )

    def transform_y(c):
        def piece(j):
            both = jnp.dot(summed[...], ty[j], preferred_element_type=jnp.float32)
            re = both[:R, :COLS] - both[R:, COLS:]
            im = both[:R, COLS:] + both[R:, :COLS]
            return jnp.concatenate([re, im], axis=1).astype(jnp.bfloat16)

        def each(k, carry):
            to = (slab + k) % SLABS
            outgoing[c, to] = piece(to)
            swap(c, to).start()
            return carry
        lax.fori_loop(1, SLABS, each, 0)
        halves[slab, c] = piece(slab)

    first(0)
    partner(0)
    near(0, 0)
    near(0, 1)
    for c in range(CHUNKS):
        more = c + 1 < CHUNKS
        relay(c, 0)
        far(c, 0)
        far(c, 1)
        if more:
            first(c + 1)
        relay(c, -1)
        relay(c, 1)
        if more:
            partner(c + 1)
        relay(c, 2)
        if more:
            near(c + 1, 0)
        last(c)
        if more:
            near(c + 1, 1)
        if c == 0:
            for load in loads:
                load.wait()
        contract(c)
        transform_y(c)

    for c in range(CHUNKS):
        def each(k, carry, c=c):
            origin = (slab + k) % SLABS
            pltpu.make_async_remote_copy(
                src_ref=outgoing.at[c, origin], dst_ref=halves.at[origin, c],
                send_sem=swap_send.at[c, origin], recv_sem=swap_recv.at[c, origin],
                device_id={"kslab": origin}, device_id_type=MESH,
            ).wait_recv()
            return carry
        lax.fori_loop(1, SLABS, each, 0)

    incoming = halves[...].reshape(NX, 2 * COLS)
    for i in range(4):
        rows = pl.ds(i * 128, 128)
        low = pl.ds(NX + i * 128, 128)
        by_cos = jnp.dot(tx[rows], incoming, preferred_element_type=jnp.float32)
        by_sin = jnp.dot(tx[low], incoming, preferred_element_type=jnp.float32)
        scale = con[rows]
        out[0, 0, rows] = ((by_cos[:, :COLS] - by_sin[:, COLS:]) * scale).astype(jnp.bfloat16)
        out[0, 1, rows] = ((by_sin[:, :COLS] + by_cos[:, COLS:]) * scale).astype(jnp.bfloat16)

    for c in range(CHUNKS):
        for p in range(2):
            sent = held.at[c, p, pl.ds(0, LAYERS - 1)]
            pltpu.make_async_remote_copy(
                src_ref=sent, dst_ref=sent,
                send_sem=send_sem.at[c, p], recv_sem=recv_sem.at[c, p, 0],
                device_id={"depth": layer(0, 1, 0, 0)}, device_id_type=MESH,
            ).wait_send()

        def each(k, carry, c=c):
            swap(c, (slab + k) % SLABS).wait_send()
            return carry
        lax.fori_loop(1, SLABS, each, 0)


def on_device(spectra, green, contrast):
    cos_y, sin_y = fourier_tables(NY)
    table_y = np.stack(
        [
            np.concatenate(
                [cos_y[:, j * COLS:(j + 1) * COLS], sin_y[:, j * COLS:(j + 1) * COLS]], axis=1
            )
            for j in range(SLABS)
        ]
    )
    cos_x, sin_x = fourier_tables(NX)
    table_x = np.concatenate([cos_x, sin_x], axis=0)
    anywhere = pl.BlockSpec(memory_space=pl.ANY)
    return pl.pallas_call(
        kernel,
        out_shape=jax.ShapeDtypeStruct((1, 2, NX, COLS), jnp.bfloat16),
        in_specs=[anywhere] * 5,
        out_specs=pl.BlockSpec(memory_space=pltpu.VMEM),
        scratch_shapes=[
            pltpu.VMEM((CHUNKS, 2, LAYERS, R, NY), jnp.bfloat16),
            pltpu.VMEM((LAYERS, 2, ROWS, NY), jnp.bfloat16),
            pltpu.VMEM((SLABS, NY, 2 * COLS), jnp.bfloat16),
            pltpu.VMEM((2 * NX, NX), jnp.bfloat16),
            pltpu.VMEM((NX, COLS), jnp.float32),
            pltpu.VMEM((2 * R, NY), jnp.bfloat16),
            pltpu.VMEM((CHUNKS, SLABS, R, 2 * COLS), jnp.bfloat16),
            pltpu.VMEM((SLABS, CHUNKS, R, 2 * COLS), jnp.bfloat16),
            pltpu.SemaphoreType.DMA((CHUNKS, 2)),
            pltpu.SemaphoreType.DMA((4,)),
            pltpu.SemaphoreType.DMA((CHUNKS, 2)),
            pltpu.SemaphoreType.DMA((CHUNKS, 2, LAYERS)),
            pltpu.SemaphoreType.DMA((CHUNKS, SLABS)),
            pltpu.SemaphoreType.DMA((CHUNKS, SLABS)),
        ],
        compiler_params=pltpu.CompilerParams(
            collective_id=0, has_side_effects=True, vmem_limit_bytes=48 * 1024 * 1024
        ),
    )(spectra, green, contrast, jnp.asarray(table_y), jnp.asarray(table_x))


def solution(mesh):
    in_specs = (
        P("depth", None, "kslab", None),
        P("depth", None, None, "kslab", None),
        P("depth", None, "kslab"),
    )
    out_specs = P("depth", None, None, "kslab")
    return jax.shard_map(
        on_device, mesh=mesh, in_specs=in_specs, out_specs=out_specs, check_vma=False
    )
```

```python
import functools
import math

import jax
import jax.numpy as jnp
import ml_dtypes
import numpy as np
from jax import lax
from jax.experimental import pallas as pl
from jax.experimental.pallas import tpu as pltpu
from jax.sharding import PartitionSpec as P

NX = 512
NY = 1024
LAYERS = 32
SLABS = 8
ROWS = NX // SLABS
COLS = NY // SLABS
PIECES = 4
R = ROWS // PIECES
CHUNKS = PIECES // 2
WIDE = 256
CROSSINGS = (6, 6)
MESH = pl.DeviceIdType.MESH


def fourier_tables(length):
    indices = np.arange(length, dtype=np.int64)
    products = indices[:, None] * indices[None, :] % length
    angles = products.astype(np.float64) * (2.0 * math.pi / length)
    factor = 1.0 / math.sqrt(length)
    return (
        (np.cos(angles) * factor).astype(np.float32).astype(ml_dtypes.bfloat16),
        (np.sin(angles) * factor).astype(np.float32).astype(ml_dtypes.bfloat16),
    )


def kernel(
    spectra, green, contrast, table_y, table_x, out,
    held, coeffs, ty, tx, con, partial, summed, outgoing, halves,
    own_sem, load_sem, send_sem, recv_sem, swap_send, swap_recv,
):
    depth = lax.axis_index("depth")
    slab = lax.axis_index("kslab")
    at_x, at_y, at_z = depth // 8, (depth // 2) % 4, depth % 2

    def own_copy(g):
        return pltpu.make_async_copy(
            spectra.at[0, :, pl.ds(g * R, R)], held.at[g, depth], own_sem.at[g]
        )

    for g in range(PIECES):
        own_copy(g).start()

    def layer(h, dz, da, db):
        ca = at_x * (1 - h) + at_y * h
        cb = at_y * (1 - h) + at_x * h
        return (
            (ca + da + 4) % 4 * (8 - 6 * h)
            + (cb + db + 4) % 4 * (2 + 6 * h)
            + (at_z + dz) % 2
        )

    barrier = pltpu.get_barrier_semaphore()
    for other in (
        layer(0, 1, 0, 0), layer(0, 0, 1, 0), layer(0, 0, -1, 0),
        layer(0, 0, 0, 1), layer(0, 0, 0, -1),
    ):
        pl.semaphore_signal(
            barrier, inc=1, device_id={"depth": other}, device_id_type=MESH
        )
    for k in range(1, SLABS):
        pl.semaphore_signal(
            barrier, inc=1, device_id={"kslab": (slab + k) % SLABS}, device_id_type=MESH
        )
    pl.semaphore_wait(barrier, 5 + SLABS - 1)

    def send(g, block, to, half=None):
        ref = held.at[g, block] if half is None else held.at[g, block, half]
        pltpu.make_async_remote_copy(
            src_ref=ref, dst_ref=ref,
            send_sem=send_sem.at[g], recv_sem=recv_sem.at[g, block],
            device_id={"depth": to}, device_id_type=MESH,
        ).start()

    def arrived(g, block):
        ref = held.at[g, block]
        pltpu.make_async_remote_copy(
            src_ref=ref, dst_ref=ref,
            send_sem=send_sem.at[g], recv_sem=recv_sem.at[g, block],
            device_id={"depth": layer(0, 1, 0, 0)}, device_id_type=MESH,
        ).wait_recv()

    def across(g, h, block):
        send(g, block, layer(h, 1, 0, 0))

    def along_a(g, h, block):
        send(g, block, layer(h, 0, 1, 0))
        send(g, block, layer(h, 0, -1, 0))

    def along_b(g, h, block):
        send(g, block, layer(h, 0, 0, 1))
        send(g, block, layer(h, 0, 0, -1))

    def both(c, step):
        def body(h, carry):
            step(2 * c + h, h)
            return carry
        lax.fori_loop(0, 2, body, 0)

    def own(c):
        def step(g, h):
            own_copy(g).wait()
            across(g, h, depth)
            along_a(g, h, depth)
        both(c, step)
        both(c, lambda g, h: along_b(g, h, depth))

    def partner(c):
        def step(g, h):
            block = layer(h, 1, 0, 0)
            arrived(g, block)
            if CROSSINGS[c] == 1:
                along_a(g, h, block)
            if CROSSINGS[c] < 6:
                along_b(g, h, block)
        both(c, step)

    def near(c, dz):
        def step(g, h):
            before, after = layer(h, dz, -1, 0), layer(h, dz, 1, 0)
            in_plane = dz == 0 or CROSSINGS[c] == 1
            arrived(g, before)
            if in_plane:
                send(g, before, layer(h, 0, 1, 0), 0)
            arrived(g, after)
            if in_plane:
                send(g, after, layer(h, 0, -1, 0), 1)
            if dz == 0 and CROSSINGS[c] > 1:
                across(g, h, before)
                across(g, h, after)
            along_b(g, h, before)
            along_b(g, h, after)
        both(c, step)

    def far(c, dz):
        def step(g, h):
            block = layer(h, dz, 2, 0)
            arrived(g, block)
            if dz == 0 and CROSSINGS[c] > 1:
                across(g, h, block)
            along_b(g, h, block)
        both(c, step)

    def relay(c, dz, da):
        def step(g, h):
            before, after = layer(h, dz, da, -1), layer(h, dz, da, 1)
            arrived(g, before)
            send(g, before, layer(h, 0, 0, 1), 0)
            arrived(g, after)
            send(g, after, layer(h, 0, 0, -1), 1)
            if dz == 0 and da == 0 and CROSSINGS[c] == 6:
                across(g, h, before)
                across(g, h, after)
        both(c, step)

    def last(c, dz):
        def step(g, h):
            for da in range(4):
                arrived(g, layer(h, dz, da, 2))
        both(c, step)

    def contract(c, offsets, start=False, end=False):
        def step(g, h):
            rows = pl.ds(pl.multiple_of(g * R, R), R)
            blocks = [layer(h, *offset) for offset in offsets]

            def column(j, carry):
                cs = pl.ds(pl.multiple_of(j * WIDE, WIDE), WIDE)
                re = None if start else partial[h, 0, :, cs]
                im = None if start else partial[h, 1, :, cs]
                for s in blocks:
                    gr = coeffs[s, 0, rows, cs].astype(jnp.float32)
                    gi = coeffs[s, 1, rows, cs].astype(jnp.float32)
                    xr = held[g, s, 0, :, cs].astype(jnp.float32)
                    xi = held[g, s, 1, :, cs].astype(jnp.float32)
                    more_re = gr * xr - gi * xi
                    more_im = gr * xi + gi * xr
                    re = more_re if re is None else re + more_re
                    im = more_im if im is None else im + more_im
                if end:
                    at = pl.multiple_of(h * R, R)
                    summed[pl.ds(at, R), cs] = re.astype(jnp.bfloat16)
                    summed[pl.ds(2 * R + at, R), cs] = im.astype(jnp.bfloat16)
                else:
                    partial[h, 0, :, cs] = re
                    partial[h, 1, :, cs] = im
                return carry
            lax.fori_loop(0, NY // WIDE, column, 0)
        both(c, step)

    def swap(c, to):
        return pltpu.make_async_remote_copy(
            src_ref=outgoing.at[c, to], dst_ref=halves.at[slab, c],
            send_sem=swap_send.at[c, to], recv_sem=swap_recv.at[c, slab],
            device_id={"kslab": to}, device_id_type=MESH,
        )

    def transform_y(c):
        def piece(j):
            both = jnp.dot(summed[...], ty[j], preferred_element_type=jnp.float32)
            re = both[:2 * R, :COLS] - both[2 * R:, COLS:]
            im = both[:2 * R, COLS:] + both[2 * R:, :COLS]
            return jnp.concatenate([re, im], axis=1).astype(jnp.bfloat16)

        def each(k, carry):
            to = (slab + k) % SLABS
            outgoing[c, to] = piece(to)
            swap(c, to).start()
            return carry
        lax.fori_loop(1, SLABS, each, 0)
        halves[slab, c] = piece(slab)

    loads = [
        pltpu.make_async_copy(green.at[0], coeffs, load_sem.at[0]),
        pltpu.make_async_copy(table_y, ty, load_sem.at[1]),
        pltpu.make_async_copy(table_x, tx, load_sem.at[2]),
        pltpu.make_async_copy(contrast.at[0], con, load_sem.at[3]),
    ]

    def start_loads():
        for load in loads:
            load.start()

    def wait_loads():
        for load in loads:
            load.wait()

    early0 = [(0, da, db) for da in (0, 1, -1, 2) for db in (0, 1, -1)]
    early1 = [(1, da, db) for da in (0, 1, -1, 2) for db in (0, 1, -1)]
    late0 = [(0, da, 2) for da in range(4)]
    late1 = [(1, da, 2) for da in range(4)]

    own(0)
    start_loads()
    near(0, 0)
    partner(0)
    far(0, 0)
    relay(0, 0, 0)
    near(0, 1)
    own(1)
    relay(0, 0, 1)
    relay(0, 0, -1)
    far(0, 1)
    near(1, 0)
    relay(0, 0, 2)
    relay(0, 1, 1)
    relay(0, 1, -1)
    wait_loads()
    contract(0, early0, start=True)
    partner(1)
    far(1, 0)
    relay(0, 1, 0)
    relay(0, 1, 2)
    relay(1, 0, 0)
    contract(0, early1)
    near(1, 1)
    last(0, 0)
    contract(0, late0)
    last(0, 1)
    contract(0, late1, end=True)
    relay(1, 0, 1)
    relay(1, 0, -1)
    far(1, 1)
    transform_y(0)
    relay(1, 0, 2)
    relay(1, 1, 1)
    relay(1, 1, -1)
    contract(1, early0, start=True)
    relay(1, 1, 0)
    relay(1, 1, 2)
    contract(1, early1)
    last(1, 0)
    contract(1, late0)
    last(1, 1)
    contract(1, late1, end=True)
    transform_y(1)

    for c in range(CHUNKS):
        def each(k, carry, c=c):
            origin = (slab + k) % SLABS
            pltpu.make_async_remote_copy(
                src_ref=outgoing.at[c, origin], dst_ref=halves.at[origin, c],
                send_sem=swap_send.at[c, origin], recv_sem=swap_recv.at[c, origin],
                device_id={"kslab": origin}, device_id_type=MESH,
            ).wait_recv()
            return carry
        lax.fori_loop(1, SLABS, each, 0)

    incoming = halves[...].reshape(NX, 2 * COLS)
    for i in range(4):
        rows = pl.ds(i * 128, 128)
        low = pl.ds(NX + i * 128, 128)
        by_cos = jnp.dot(tx[rows], incoming, preferred_element_type=jnp.float32)
        by_sin = jnp.dot(tx[low], incoming, preferred_element_type=jnp.float32)
        scale = con[rows]
        out[0, 0, rows] = ((by_cos[:, :COLS] - by_sin[:, COLS:]) * scale).astype(jnp.bfloat16)
        out[0, 1, rows] = ((by_sin[:, :COLS] + by_cos[:, COLS:]) * scale).astype(jnp.bfloat16)

    for g in range(PIECES):
        sent = held.at[g, pl.ds(0, LAYERS - 1)]
        pltpu.make_async_remote_copy(
            src_ref=sent, dst_ref=sent,
            send_sem=send_sem.at[g], recv_sem=recv_sem.at[g, 0],
            device_id={"depth": layer(0, 1, 0, 0)}, device_id_type=MESH,
        ).wait_send()
    for c in range(CHUNKS):
        def each(k, carry, c=c):
            swap(c, (slab + k) % SLABS).wait_send()
            return carry
        lax.fori_loop(1, SLABS, each, 0)


def on_device(spectra, green, contrast):
    cos_y, sin_y = fourier_tables(NY)
    table_y = np.stack(
        [
            np.concatenate(
                [cos_y[:, j * COLS:(j + 1) * COLS], sin_y[:, j * COLS:(j + 1) * COLS]], axis=1
            )
            for j in range(SLABS)
        ]
    )
    cos_x, sin_x = fourier_tables(NX)
    table_x = np.concatenate([cos_x, sin_x], axis=0)
    anywhere = pl.BlockSpec(memory_space=pl.ANY)
    return pl.pallas_call(
        kernel,
        out_shape=jax.ShapeDtypeStruct((1, 2, NX, COLS), jnp.bfloat16),
        in_specs=[anywhere] * 5,
        out_specs=pl.BlockSpec(memory_space=pltpu.VMEM),
        scratch_shapes=[
            pltpu.VMEM((PIECES, LAYERS, 2, R, NY), jnp.bfloat16),
            pltpu.VMEM((LAYERS, 2, ROWS, NY), jnp.bfloat16),
            pltpu.VMEM((SLABS, NY, 2 * COLS), jnp.bfloat16),
            pltpu.VMEM((2 * NX, NX), jnp.bfloat16),
            pltpu.VMEM((NX, COLS), jnp.float32),
            pltpu.VMEM((2, 2, R, NY), jnp.float32),
            pltpu.VMEM((4 * R, NY), jnp.bfloat16),
            pltpu.VMEM((CHUNKS, SLABS, 2 * R, 2 * COLS), jnp.bfloat16),
            pltpu.VMEM((SLABS, CHUNKS, 2 * R, 2 * COLS), jnp.bfloat16),
            pltpu.SemaphoreType.DMA((PIECES,)),
            pltpu.SemaphoreType.DMA((4,)),
            pltpu.SemaphoreType.DMA((PIECES,)),
            pltpu.SemaphoreType.DMA((PIECES, LAYERS)),
            pltpu.SemaphoreType.DMA((CHUNKS, SLABS)),
            pltpu.SemaphoreType.DMA((CHUNKS, SLABS)),
        ],
        compiler_params=pltpu.CompilerParams(
            collective_id=0, has_side_effects=True, vmem_limit_bytes=60 * 1024 * 1024
        ),
    )(spectra, green, contrast, jnp.asarray(table_y), jnp.asarray(table_x))


def solution(mesh):
    in_specs = (
        P("depth", None, "kslab", None),
        P("depth", None, None, "kslab", None),
        P("depth", None, "kslab"),
    )
    out_specs = P("depth", None, None, "kslab")
    return jax.shard_map(
        on_device, mesh=mesh, in_specs=in_specs, out_specs=out_specs, check_vma=False
    )
```

```python
import functools
import math

import jax
import jax.numpy as jnp
import ml_dtypes
import numpy as np
from jax import lax
from jax.experimental import pallas as pl
from jax.experimental.pallas import tpu as pltpu
from jax.sharding import PartitionSpec as P

NX = 512
NY = 1024
LAYERS = 32
SLABS = 8
ROWS = NX // SLABS
COLS = NY // SLABS
PIECES = 4
R = ROWS // PIECES
CHUNKS = PIECES // 2
WIDE = 256
CROSSINGS = (6, 6)
MESH = pl.DeviceIdType.MESH


def fourier_tables(length):
    indices = np.arange(length, dtype=np.int64)
    products = indices[:, None] * indices[None, :] % length
    angles = products.astype(np.float64) * (2.0 * math.pi / length)
    factor = 1.0 / math.sqrt(length)
    return (
        (np.cos(angles) * factor).astype(np.float32).astype(ml_dtypes.bfloat16),
        (np.sin(angles) * factor).astype(np.float32).astype(ml_dtypes.bfloat16),
    )


def kernel(
    spectra, green, contrast, table_y, table_x, out,
    held, coeffs, ty, tx, con, partial, summed, outgoing, halves,
    own_sem, load_sem, send_sem, recv_sem, swap_send, swap_recv,
):
    depth = lax.axis_index("depth")
    slab = lax.axis_index("kslab")
    at_x, at_y, at_z = depth // 8, (depth // 2) % 4, depth % 2

    def own_copy(g):
        return pltpu.make_async_copy(
            spectra.at[0, :, pl.ds(g * R, R)], held.at[g, depth], own_sem.at[g]
        )

    for g in range(PIECES):
        own_copy(g).start()

    def layer(h, dz, da, db):
        ca = at_x * (1 - h) + at_y * h
        cb = at_y * (1 - h) + at_x * h
        return (
            (ca + da + 4) % 4 * (8 - 6 * h)
            + (cb + db + 4) % 4 * (2 + 6 * h)
            + (at_z + dz) % 2
        )

    barrier = pltpu.get_barrier_semaphore()
    for other in (
        layer(0, 1, 0, 0), layer(0, 0, 1, 0), layer(0, 0, -1, 0),
        layer(0, 0, 0, 1), layer(0, 0, 0, -1),
    ):
        pl.semaphore_signal(
            barrier, inc=1, device_id={"depth": other}, device_id_type=MESH
        )
    for k in range(1, SLABS):
        pl.semaphore_signal(
            barrier, inc=1, device_id={"kslab": (slab + k) % SLABS}, device_id_type=MESH
        )
    pl.semaphore_wait(barrier, 5 + SLABS - 1)

    def send(g, block, to, half=None):
        ref = held.at[g, block] if half is None else held.at[g, block, half]
        pltpu.make_async_remote_copy(
            src_ref=ref, dst_ref=ref,
            send_sem=send_sem.at[g], recv_sem=recv_sem.at[g, block],
            device_id={"depth": to}, device_id_type=MESH,
        ).start()

    def arrived(g, block):
        ref = held.at[g, block]
        pltpu.make_async_remote_copy(
            src_ref=ref, dst_ref=ref,
            send_sem=send_sem.at[g], recv_sem=recv_sem.at[g, block],
            device_id={"depth": layer(0, 1, 0, 0)}, device_id_type=MESH,
        ).wait_recv()

    def across(g, h, block):
        send(g, block, layer(h, 1, 0, 0))

    def along_a(g, h, block):
        send(g, block, layer(h, 0, 1, 0))
        send(g, block, layer(h, 0, -1, 0))

    def along_b(g, h, block):
        send(g, block, layer(h, 0, 0, 1))
        send(g, block, layer(h, 0, 0, -1))

    def both(c, step):
        def body(h, carry):
            step(2 * c + h, h)
            return carry
        lax.fori_loop(0, 2, body, 0)

    def own(c):
        def step(g, h):
            own_copy(g).wait()
            across(g, h, depth)
            along_a(g, h, depth)
        both(c, step)
        both(c, lambda g, h: along_b(g, h, depth))

    def partner(c):
        def step(g, h):
            block = layer(h, 1, 0, 0)
            arrived(g, block)
            if CROSSINGS[c] == 1:
                along_a(g, h, block)
            if CROSSINGS[c] < 6:
                along_b(g, h, block)
        both(c, step)

    def near(c, dz):
        def step(g, h):
            before, after = layer(h, dz, -1, 0), layer(h, dz, 1, 0)
            in_plane = dz == 0 or CROSSINGS[c] == 1
            arrived(g, before)
            if in_plane:
                send(g, before, layer(h, 0, 1, 0), 0)
            arrived(g, after)
            if in_plane:
                send(g, after, layer(h, 0, -1, 0), 1)
            if dz == 0 and CROSSINGS[c] > 1:
                across(g, h, before)
                across(g, h, after)
            along_b(g, h, before)
            along_b(g, h, after)
        both(c, step)

    def far(c, dz):
        def step(g, h):
            block = layer(h, dz, 2, 0)
            arrived(g, block)
            if dz == 0 and CROSSINGS[c] > 1:
                across(g, h, block)
            along_b(g, h, block)
        both(c, step)

    def relay(c, dz, da):
        def step(g, h):
            before, after = layer(h, dz, da, -1), layer(h, dz, da, 1)
            arrived(g, before)
            send(g, before, layer(h, 0, 0, 1), 0)
            arrived(g, after)
            send(g, after, layer(h, 0, 0, -1), 1)
            if dz == 0 and da == 0 and CROSSINGS[c] == 6:
                across(g, h, before)
                across(g, h, after)
        both(c, step)

    def last(c, dz):
        def step(g, h):
            for da in range(4):
                arrived(g, layer(h, dz, da, 2))
        both(c, step)

    def contract(c, offsets, start=False, end=False):
        def step(g, h):
            rows = pl.ds(pl.multiple_of(g * R, R), R)
            blocks = [layer(h, *offset) for offset in offsets]

            def column(j, carry):
                cs = pl.ds(pl.multiple_of(j * WIDE, WIDE), WIDE)
                re = None if start else partial[h, 0, :, cs]
                im = None if start else partial[h, 1, :, cs]
                for s in blocks:
                    gr = coeffs[s, 0, rows, cs].astype(jnp.float32)
                    gi = coeffs[s, 1, rows, cs].astype(jnp.float32)
                    xr = held[g, s, 0, :, cs].astype(jnp.float32)
                    xi = held[g, s, 1, :, cs].astype(jnp.float32)
                    more_re = gr * xr - gi * xi
                    more_im = gr * xi + gi * xr
                    re = more_re if re is None else re + more_re
                    im = more_im if im is None else im + more_im
                if end:
                    at = pl.multiple_of(h * R, R)
                    summed[pl.ds(at, R), cs] = re.astype(jnp.bfloat16)
                    summed[pl.ds(2 * R + at, R), cs] = im.astype(jnp.bfloat16)
                else:
                    partial[h, 0, :, cs] = re
                    partial[h, 1, :, cs] = im
                return carry
            lax.fori_loop(0, NY // WIDE, column, 0)
        both(c, step)

    def swap(c, to):
        return pltpu.make_async_remote_copy(
            src_ref=outgoing.at[c, to], dst_ref=halves.at[slab, c],
            send_sem=swap_send.at[c, to], recv_sem=swap_recv.at[c, slab],
            device_id={"kslab": to}, device_id_type=MESH,
        )

    def peer(k):
        pair = k // 2
        ahead = (2 + pair % 2) * (1 - pair // 2) + (1 - pair % 2) * (pair // 2)
        chip = (slab // 2 + ahead) % 4
        return chip * 2 + (slab + 1 + k) % 2

    def transform_y(c):
        def pair(k):
            tables = [ty[peer(2 * k)], ty[peer(2 * k + 1)]]
            result = []
            for table in tables:
                both = jnp.dot(summed[...], table, preferred_element_type=jnp.float32)
                re = both[:2 * R, :COLS] - both[2 * R:, COLS:]
                im = both[:2 * R, COLS:] + both[2 * R:, :COLS]
                result.append(jnp.concatenate([re, im], axis=1).astype(jnp.bfloat16))
            return result

        def each(k, carry):
            one, two = pair(k)
            outgoing[c, peer(2 * k)] = one
            swap(c, peer(2 * k)).start()
            outgoing[c, peer(2 * k + 1)] = two
            swap(c, peer(2 * k + 1)).start()
            return carry
        lax.fori_loop(0, SLABS // 2 - 1, each, 0)
        one, two = pair(SLABS // 2 - 1)
        outgoing[c, peer(SLABS - 2)] = one
        swap(c, peer(SLABS - 2)).start()
        halves[slab, c] = two

    loads = [
        pltpu.make_async_copy(green.at[0], coeffs, load_sem.at[0]),
        pltpu.make_async_copy(table_y, ty, load_sem.at[1]),
        pltpu.make_async_copy(table_x, tx, load_sem.at[2]),
        pltpu.make_async_copy(contrast.at[0], con, load_sem.at[3]),
    ]

    def start_loads():
        for load in loads:
            load.start()

    def wait_loads():
        for load in loads:
            load.wait()

    early0 = [(0, da, db) for da in (0, 1, -1, 2) for db in (0, 1, -1)]
    early1 = [(1, da, db) for da in (0, 1, -1, 2) for db in (0, 1, -1)]
    late0 = [(0, da, 2) for da in range(4)]
    late1 = [(1, da, 2) for da in range(4)]

    own(0)
    start_loads()
    own(1)
    near(0, 0)
    near(1, 0)
    relay(0, 0, 1)
    near(0, 1)
    far(0, 0)
    partner(0)
    relay(0, 0, 0)
    partner(1)
    relay(0, 0, -1)
    relay(0, 1, 1)
    far(1, 0)
    relay(0, 0, 2)
    far(0, 1)
    near(1, 1)
    relay(0, 1, 2)
    wait_loads()
    contract(0, early0, start=True)
    relay(0, 1, 0)
    relay(0, 1, -1)
    last(0, 0)
    relay(1, 0, -1)
    relay(1, 0, 0)
    relay(1, 0, 1)
    relay(1, 0, 2)
    contract(0, early1)
    last(0, 1)
    contract(0, late0)
    far(1, 1)
    contract(0, late1, end=True)
    relay(1, 1, 1)
    contract(1, early0, start=True)
    relay(1, 1, -1)
    transform_y(0)
    relay(1, 1, 2)
    last(1, 0)
    relay(1, 1, 0)
    contract(1, early1)
    contract(1, late0)
    last(1, 1)
    contract(1, late1, end=True)
    transform_y(1)

    for c in range(CHUNKS):
        def each(k, carry, c=c):
            origin = (slab + k) % SLABS
            pltpu.make_async_remote_copy(
                src_ref=outgoing.at[c, origin], dst_ref=halves.at[origin, c],
                send_sem=swap_send.at[c, origin], recv_sem=swap_recv.at[c, origin],
                device_id={"kslab": origin}, device_id_type=MESH,
            ).wait_recv()
            return carry
        lax.fori_loop(1, SLABS, each, 0)

    incoming = halves[...].reshape(NX, 2 * COLS)
    for i in range(4):
        rows = pl.ds(i * 128, 128)
        low = pl.ds(NX + i * 128, 128)
        by_cos = jnp.dot(tx[rows], incoming, preferred_element_type=jnp.float32)
        by_sin = jnp.dot(tx[low], incoming, preferred_element_type=jnp.float32)
        scale = con[rows]
        out[0, 0, rows] = ((by_cos[:, :COLS] - by_sin[:, COLS:]) * scale).astype(jnp.bfloat16)
        out[0, 1, rows] = ((by_sin[:, :COLS] + by_cos[:, COLS:]) * scale).astype(jnp.bfloat16)

    for g in range(PIECES):
        sent = held.at[g, pl.ds(0, LAYERS - 1)]
        pltpu.make_async_remote_copy(
            src_ref=sent, dst_ref=sent,
            send_sem=send_sem.at[g], recv_sem=recv_sem.at[g, 0],
            device_id={"depth": layer(0, 1, 0, 0)}, device_id_type=MESH,
        ).wait_send()
    for c in range(CHUNKS):
        def each(k, carry, c=c):
            swap(c, (slab + k) % SLABS).wait_send()
            return carry
        lax.fori_loop(1, SLABS, each, 0)


def on_device(spectra, green, contrast):
    cos_y, sin_y = fourier_tables(NY)
    table_y = np.stack(
        [
            np.concatenate(
                [cos_y[:, j * COLS:(j + 1) * COLS], sin_y[:, j * COLS:(j + 1) * COLS]], axis=1
            )
            for j in range(SLABS)
        ]
    )
    cos_x, sin_x = fourier_tables(NX)
    table_x = np.concatenate([cos_x, sin_x], axis=0)
    anywhere = pl.BlockSpec(memory_space=pl.ANY)
    return pl.pallas_call(
        kernel,
        out_shape=jax.ShapeDtypeStruct((1, 2, NX, COLS), jnp.bfloat16),
        in_specs=[anywhere] * 5,
        out_specs=pl.BlockSpec(memory_space=pltpu.VMEM),
        scratch_shapes=[
            pltpu.VMEM((PIECES, LAYERS, 2, R, NY), jnp.bfloat16),
            pltpu.VMEM((LAYERS, 2, ROWS, NY), jnp.bfloat16),
            pltpu.VMEM((SLABS, NY, 2 * COLS), jnp.bfloat16),
            pltpu.VMEM((2 * NX, NX), jnp.bfloat16),
            pltpu.VMEM((NX, COLS), jnp.float32),
            pltpu.VMEM((2, 2, R, NY), jnp.float32),
            pltpu.VMEM((4 * R, NY), jnp.bfloat16),
            pltpu.VMEM((CHUNKS, SLABS, 2 * R, 2 * COLS), jnp.bfloat16),
            pltpu.VMEM((SLABS, CHUNKS, 2 * R, 2 * COLS), jnp.bfloat16),
            pltpu.SemaphoreType.DMA((PIECES,)),
            pltpu.SemaphoreType.DMA((4,)),
            pltpu.SemaphoreType.DMA((PIECES,)),
            pltpu.SemaphoreType.DMA((PIECES, LAYERS)),
            pltpu.SemaphoreType.DMA((CHUNKS, SLABS)),
            pltpu.SemaphoreType.DMA((CHUNKS, SLABS)),
        ],
        compiler_params=pltpu.CompilerParams(
            collective_id=0, has_side_effects=True, vmem_limit_bytes=44 * 1024 * 1024
        ),
    )(*[
        pltpu.with_memory_space_constraint(operand, pltpu.MemorySpace.HBM)
        for operand in (spectra, green, contrast, jnp.asarray(table_y), jnp.asarray(table_x))
    ])


def solution(mesh):
    in_specs = (
        P("depth", None, "kslab", None),
        P("depth", None, None, "kslab", None),
        P("depth", None, "kslab"),
    )
    out_specs = P("depth", None, None, "kslab")
    return jax.shard_map(
        on_device, mesh=mesh, in_specs=in_specs, out_specs=out_specs, check_vma=False
    )
```

```python
import math

import jax
import jax.numpy as jnp
import ml_dtypes
import numpy as np
from jax import lax
from jax.experimental import pallas as pl
from jax.experimental.pallas import tpu as pltpu
from jax.sharding import PartitionSpec as P

NX = 512
NY = 1024
LAYERS = 32
SLABS = 8
ROWS = NX // SLABS
COLS = NY // SLABS
TILE = 16
SIZES = (32, 32)
STARTS = tuple(sum(SIZES[:c]) for c in range(len(SIZES)))
CHUNKS = len(SIZES)
CROSSINGS = (6, 6)
WIDE = 512
LAST = ((-1, 1), (2, 0))
GROUPS = ((0, 1), (2, 3, 4, 5, 6, 7))
MESH = pl.DeviceIdType.MESH


def fourier_tables(length):
    indices = np.arange(length, dtype=np.int64)
    products = indices[:, None] * indices[None, :] % length
    angles = products.astype(np.float64) * (2.0 * math.pi / length)
    factor = 1.0 / math.sqrt(length)
    return (
        (np.cos(angles) * factor).astype(np.float32).astype(ml_dtypes.bfloat16),
        (np.sin(angles) * factor).astype(np.float32).astype(ml_dtypes.bfloat16),
    )


def width(c):
    return NY * SIZES[c] // (2 * TILE)


def corner(c, h):
    if SIZES[c] == 2 * TILE:
        return STARTS[c] + h * TILE, h * TILE, 0
    return STARTS[c], 0, h * width(c)


def slot(dz, da, db):
    return dz % 2 * 16 + da % 4 * 4 + db % 4


def kernel(spectra, green, contrast, table_y, table_x, out, coeffs, ty, tx, con, partial, summed,
           gathered, own_sem, load_sem, send_sem, recv_sem, swap_send, swap_recv, *buffers):
    held, outgoing, halves = buffers[:CHUNKS], buffers[CHUNKS:2 * CHUNKS], buffers[2 * CHUNKS:]
    depth = lax.axis_index("depth")
    slab = lax.axis_index("kslab")
    at_x, at_y, at_z = depth // 8, (depth // 2) % 4, depth % 2

    def own_copy(c, h):
        row, _, col = corner(c, h)
        return pltpu.make_async_copy(
            spectra.at[0, :, pl.ds(row, TILE), pl.ds(col, width(c))],
            held[c].at[h, 0],
            own_sem.at[c, h],
        )

    def layer(h, dz, da, db):
        dx, dy = (da, db) if h == 0 else (db, da)
        return (at_x + dx + 4) % 4 * 8 + (at_y + dy + 4) % 4 * 2 + (at_z + dz) % 2

    ahead = (layer(0, 0, 1, 0), layer(0, 0, 0, 1))
    behind = (layer(0, 0, -1, 0), layer(0, 0, 0, -1))
    opposite = layer(0, 1, 0, 0)

    barrier = pltpu.get_barrier_semaphore()
    for other in ahead + behind + (opposite,):
        pl.semaphore_signal(
            barrier, inc=1, device_id={"depth": other}, device_id_type=MESH
        )
    for k in range(1, SLABS):
        pl.semaphore_signal(
            barrier, inc=1, device_id={"kslab": (slab + k) % SLABS}, device_id_type=MESH
        )
    for c in range(CHUNKS):
        for h in range(2):
            own_copy(c, h).start()

    pl.semaphore_wait(barrier, 5 + SLABS - 1)

    def send(c, h, offset, axis, step, half=None):
        dz, da, db = offset
        if axis == "z":
            there, to = slot(dz + 1, da, db), opposite
        else:
            at = h if axis == "a" else 1 - h
            to = ahead[at] if step > 0 else behind[at]
            there = slot(dz, da - step, db) if axis == "a" else slot(dz, da, db - step)
        source, target = held[c].at[h, slot(*offset)], held[c].at[h, there]
        if half is not None:
            source, target = held[c].at[h, slot(*offset), half], held[c].at[h, there, half]
        pltpu.make_async_remote_copy(
            src_ref=source, dst_ref=target,
            send_sem=send_sem.at[c, h], recv_sem=recv_sem.at[c, h, there],
            device_id={"depth": to}, device_id_type=MESH,
        ).start()

    def arrived(c, h, *offset):
        ref = held[c].at[h, slot(*offset)]
        pltpu.make_async_remote_copy(
            src_ref=ref, dst_ref=ref,
            send_sem=send_sem.at[c, h], recv_sem=recv_sem.at[c, h, slot(*offset)],
            device_id={"depth": opposite}, device_id_type=MESH,
        ).wait_recv()

    def along(c, h, axis, *offset):
        send(c, h, offset, axis, 1)
        send(c, h, offset, axis, -1)

    def own(c):
        for h in range(2):
            own_copy(c, h).wait()
            send(c, h, (0, 0, 0), "z", 1)
            along(c, h, "a", 0, 0, 0)
        for h in range(2):
            along(c, h, "b", 0, 0, 0)

    def partner(c):
        for h in range(2):
            arrived(c, h, 1, 0, 0)
            if CROSSINGS[c] == 1:
                along(c, h, "a", 1, 0, 0)
            if CROSSINGS[c] < 6:
                along(c, h, "b", 1, 0, 0)

    def near(c, dz):
        in_plane = dz == 0 or CROSSINGS[c] == 1
        for h in range(2):
            arrived(c, h, dz, -1, 0)
            if in_plane:
                send(c, h, (dz, -1, 0), "a", 1, 0)
            arrived(c, h, dz, 1, 0)
            if in_plane:
                send(c, h, (dz, 1, 0), "a", -1, 1)
            if dz == 0 and CROSSINGS[c] > 1:
                send(c, h, (0, -1, 0), "z", 1)
                send(c, h, (0, 1, 0), "z", 1)
            along(c, h, "b", dz, -1, 0)
            along(c, h, "b", dz, 1, 0)

    def far(c, dz):
        for h in range(2):
            arrived(c, h, dz, 2, 0)
            if dz == 0 and CROSSINGS[c] > 1:
                send(c, h, (0, 2, 0), "z", 1)
            along(c, h, "b", dz, 2, 0)

    def relay(c, dz, da):
        for h in range(2):
            arrived(c, h, dz, da, -1)
            send(c, h, (dz, da, -1), "b", 1, 0)
            arrived(c, h, dz, da, 1)
            send(c, h, (dz, da, 1), "b", -1, 1)
            if dz == 0 and da == 0 and CROSSINGS[c] == 6:
                send(c, h, (0, 0, -1), "z", 1)
                send(c, h, (0, 0, 1), "z", 1)

    def last(c, dz):
        for h in range(2):
            for da in range(4):
                arrived(c, h, dz, da, 2)

    def contract(c, offsets, start=False, end=False, parts=(0, 1)):
        for h in parts:
            row, low, col = corner(c, h)
            layers = [layer(h, *offset) for offset in offsets]
            slots = [slot(*offset) for offset in offsets]

            def column(j, carry, h=h, row=row, low=low, col=col, layers=layers, slots=slots):
                cs = pl.ds(pl.multiple_of(j * WIDE, WIDE), WIDE)
                wide = pl.ds(pl.multiple_of(col + j * WIDE, WIDE), WIDE)
                here = pl.ds(low, TILE)
                re = None if start else partial[0, here, wide]
                im = None if start else partial[1, here, wide]
                for s, k in zip(layers, slots):
                    gr = coeffs[s, 0, pl.ds(row, TILE), wide].astype(jnp.float32)
                    gi = coeffs[s, 1, pl.ds(row, TILE), wide].astype(jnp.float32)
                    xr = held[c][h, k, 0, :, cs].astype(jnp.float32)
                    xi = held[c][h, k, 1, :, cs].astype(jnp.float32)
                    more_re = gr * xr - gi * xi
                    more_im = gr * xi + gi * xr
                    re = more_re if re is None else re + more_re
                    im = more_im if im is None else im + more_im
                if end:
                    summed[here, wide] = re.astype(jnp.bfloat16)
                    summed[pl.ds(SIZES[c] + low, TILE), wide] = im.astype(jnp.bfloat16)
                else:
                    partial[0, here, wide] = re
                    partial[1, here, wide] = im
                return carry
            lax.fori_loop(0, width(c) // WIDE, column, 0)

    def finish(c):
        for at, pair in enumerate(LAST):
            for h in range(2):
                for da in pair:
                    arrived(c, h, 1, da, 2)
                offsets = [(1, da, 2) for da in pair]
                contract(c, offsets, end=at == len(LAST) - 1, parts=(h,))

    def peer(k):
        chip = (slab // 2 + (2, 3, 1, 0)[k // 2]) % 4
        return chip * 2 + (slab + 1 + k) % 2

    peers = [peer(k) for k in range(SLABS)]

    def swap(c, k):
        return pltpu.make_async_remote_copy(
            src_ref=outgoing[c].at[k], dst_ref=halves[c].at[slab],
            send_sem=swap_send.at[c, k], recv_sem=swap_recv.at[c, slab],
            device_id={"kslab": peers[k]}, device_id_type=MESH,
        )

    def transform_y(c):
        n = SIZES[c]
        for group in GROUPS:
            results = []
            for k in group:
                both = jnp.dot(summed[:2 * n], ty[peers[k]], preferred_element_type=jnp.float32)
                re = both[:n, :COLS] - both[n:, COLS:]
                im = both[:n, COLS:] + both[n:, :COLS]
                results.append(jnp.concatenate([re, im], axis=1).astype(jnp.bfloat16))
            for k, result in zip(group, results):
                if k < SLABS - 1:
                    outgoing[c][k] = result
                else:
                    halves[c][slab] = result
            for k in group:
                if k < SLABS - 1:
                    swap(c, k).start()

    def swapped(c):
        for k in reversed(range(SLABS - 1)):
            pltpu.make_async_remote_copy(
                src_ref=outgoing[c].at[k], dst_ref=halves[c].at[peers[k]],
                send_sem=swap_send.at[c, k], recv_sem=swap_recv.at[c, peers[k]],
                device_id={"kslab": peers[k]}, device_id_type=MESH,
            ).wait_recv()

    def by_table(c, rows):
        columns = pl.ds(STARTS[c] * SLABS, SIZES[c] * SLABS)
        incoming = halves[c][...].reshape(SLABS * SIZES[c], 2 * COLS)
        return jnp.dot(tx[rows, columns], incoming, preferred_element_type=jnp.float32)

    def gather_x(c):
        for i in range(8):
            rows = pl.ds(i * 128, 128)
            term = by_table(c, rows)
            gathered[rows] = term if c == 0 else gathered[rows] + term

    loads = [
        pltpu.make_async_copy(green.at[0], coeffs, load_sem.at[0]),
        pltpu.make_async_copy(table_y, ty, load_sem.at[1]),
        pltpu.make_async_copy(table_x, tx, load_sem.at[2]),
        pltpu.make_async_copy(contrast.at[0], con, load_sem.at[3]),
    ]

    def start_loads():
        for load in loads:
            load.start()

    def wait_loads():
        for load in loads:
            load.wait()

    early0 = [(0, da, db) for da in (0, 1, -1, 2) for db in (0, 1, -1)]
    early1 = [(1, da, db) for da in (0, 1, -1, 2) for db in (0, 1, -1)]
    late0 = [(0, da, 2) for da in range(4)]
    late1 = [(1, da, 2) for da in range(4)]

    own(1)
    start_loads()
    own(0)
    near(1, 0)
    partner(1)
    near(0, 0)
    near(1, 1)
    far(0, 0)
    partner(0)
    relay(0, 0, 1)
    relay(0, 0, 0)
    relay(0, 0, -1)
    near(0, 1)
    relay(0, 0, 2)
    far(1, 0)
    relay(0, 1, 1)
    far(0, 1)
    wait_loads()
    contract(0, early0, start=True)
    relay(1, 0, 0)
    relay(0, 1, 0)
    relay(0, 1, -1)
    relay(0, 1, 2)
    relay(1, 0, 2)
    far(1, 1)
    contract(0, early1)
    relay(1, 0, -1)
    last(0, 0)
    contract(0, late0)
    relay(1, 0, 1)
    relay(1, 1, -1)
    last(0, 1)
    contract(0, late1, end=True)
    relay(1, 1, 1)
    transform_y(0)
    relay(1, 1, 2)
    relay(1, 1, 0)
    last(1, 0)
    contract(1, early0, start=True)
    contract(1, early1)
    contract(1, late0)
    finish(1)
    transform_y(1)

    for c in range(CHUNKS - 1):
        swapped(c)
        gather_x(c)
    for c in range(CHUNKS):
        for h in range(2):
            sent = held[c].at[h, pl.ds(0, LAYERS - 1)]
            pltpu.make_async_remote_copy(
                src_ref=sent, dst_ref=sent,
                send_sem=send_sem.at[c, h], recv_sem=recv_sem.at[c, h, 0],
                device_id={"depth": opposite}, device_id_type=MESH,
            ).wait_send()
        for k in range(SLABS - 1):
            swap(c, k).wait_send()
    swapped(CHUNKS - 1)
    for i in range(4):
        rows = pl.ds(i * 128, 128)
        low = pl.ds(NX + i * 128, 128)
        by_cos = gathered[rows] + by_table(CHUNKS - 1, rows)
        by_sin = gathered[low] + by_table(CHUNKS - 1, low)
        scale = con[rows]
        out[0, 0, rows] = ((by_cos[:, :COLS] - by_sin[:, COLS:]) * scale).astype(jnp.bfloat16)
        out[0, 1, rows] = ((by_sin[:, :COLS] + by_cos[:, COLS:]) * scale).astype(jnp.bfloat16)


def on_device(spectra, green, contrast):
    cos_y, sin_y = fourier_tables(NY)
    table_y = np.stack(
        [
            np.concatenate(
                [cos_y[:, j * COLS:(j + 1) * COLS], sin_y[:, j * COLS:(j + 1) * COLS]], axis=1
            )
            for j in range(SLABS)
        ]
    )
    cos_x, sin_x = fourier_tables(NX)
    order = np.concatenate(
        [
            (np.arange(SLABS)[:, None] * ROWS + STARTS[c] + np.arange(SIZES[c])[None]).reshape(-1)
            for c in range(CHUNKS)
        ]
    )
    table_x = np.concatenate([cos_x, sin_x], axis=0)[:, order]
    operands = [
        pltpu.with_memory_space_constraint(operand, pltpu.MemorySpace.HBM)
        for operand in (spectra, green, contrast, jnp.asarray(table_y), jnp.asarray(table_x))
    ]
    return pl.pallas_call(
        kernel,
        out_shape=jax.ShapeDtypeStruct((1, 2, NX, COLS), jnp.bfloat16),
        in_specs=[pl.BlockSpec(memory_space=pl.ANY)] * 5,
        out_specs=pl.BlockSpec(memory_space=pltpu.VMEM),
        scratch_shapes=[
            pltpu.VMEM((LAYERS, 2, ROWS, NY), jnp.bfloat16),
            pltpu.VMEM((SLABS, NY, 2 * COLS), jnp.bfloat16),
            pltpu.VMEM((2 * NX, NX), jnp.bfloat16),
            pltpu.VMEM((NX, COLS), jnp.float32),
            pltpu.VMEM((2, 2 * TILE, NY), jnp.float32),
            pltpu.VMEM((4 * TILE, NY), jnp.bfloat16),
            pltpu.VMEM((2 * NX, 2 * COLS), jnp.float32),
            pltpu.SemaphoreType.DMA((CHUNKS, 2)),
            pltpu.SemaphoreType.DMA((4,)),
            pltpu.SemaphoreType.DMA((CHUNKS, 2)),
            pltpu.SemaphoreType.DMA((CHUNKS, 2, LAYERS)),
            pltpu.SemaphoreType.DMA((CHUNKS, SLABS)),
            pltpu.SemaphoreType.DMA((CHUNKS, SLABS)),
        ]
        + [pltpu.VMEM((2, LAYERS, 2, TILE, width(c)), jnp.bfloat16) for c in range(CHUNKS)]
        + [pltpu.VMEM((SLABS, SIZES[c], 2 * COLS), jnp.bfloat16) for c in range(CHUNKS)] * 2,
        compiler_params=pltpu.CompilerParams(
            collective_id=0, has_side_effects=True, vmem_limit_bytes=44 * 1024 * 1024
        ),
    )(*operands)


def solution(mesh):
    in_specs = (
        P("depth", None, "kslab", None),
        P("depth", None, None, "kslab", None),
        P("depth", None, "kslab"),
    )
    out_specs = P("depth", None, None, "kslab")
    return jax.shard_map(
        on_device, mesh=mesh, in_specs=in_specs, out_specs=out_specs, check_vma=False
    )
```

```python
import math

import jax
import jax.numpy as jnp
import ml_dtypes
import numpy as np
from jax import lax
from jax.experimental import pallas as pl
from jax.experimental.pallas import tpu as pltpu
from jax.sharding import PartitionSpec as P

NX = 512
NY = 1024
LAYERS = 32
SLABS = 8
ROWS = NX // SLABS
COLS = NY // SLABS
TILE = 16
SIZES = (32, 32)
STARTS = tuple(sum(SIZES[:c]) for c in range(len(SIZES)))
CHUNKS = len(SIZES)
CROSSINGS = (6, 6)
WIDE = 512
LAST = ((-1, 1), (2, 0))
GROUPS = ((0, 1), (2, 3, 4, 5), (6, 7))
MESH = pl.DeviceIdType.MESH


def fourier_tables(length):
    indices = np.arange(length, dtype=np.int64)
    products = indices[:, None] * indices[None, :] % length
    angles = products.astype(np.float64) * (2.0 * math.pi / length)
    factor = 1.0 / math.sqrt(length)
    return (
        (np.cos(angles) * factor).astype(np.float32).astype(ml_dtypes.bfloat16),
        (np.sin(angles) * factor).astype(np.float32).astype(ml_dtypes.bfloat16),
    )


def width(c):
    return NY * SIZES[c] // (2 * TILE)


def corner(c, h):
    if SIZES[c] == 2 * TILE:
        return STARTS[c] + h * TILE, h * TILE, 0
    return STARTS[c], 0, h * width(c)


def slot(dz, da, db):
    return dz % 2 * 16 + da % 4 * 4 + db % 4


def kernel(spectra, green, contrast, table_y, table_x, out, coeffs, ty, tx, con, partial, summed,
           gathered, own_sem, load_sem, send_sem, recv_sem, swap_send, swap_recv, *buffers):
    held, outgoing, halves = buffers[:CHUNKS], buffers[CHUNKS:2 * CHUNKS], buffers[2 * CHUNKS:]
    depth = lax.axis_index("depth")
    slab = lax.axis_index("kslab")
    at_x, at_y, at_z = depth // 8, (depth // 2) % 4, depth % 2

    def own_copy(c, h):
        row, _, col = corner(c, h)
        return pltpu.make_async_copy(
            spectra.at[0, :, pl.ds(row, TILE), pl.ds(col, width(c))],
            held[c].at[h, 0],
            own_sem.at[c, h],
        )

    def layer(h, dz, da, db):
        dx, dy = (da, db) if h == 0 else (db, da)
        return (at_x + dx + 4) % 4 * 8 + (at_y + dy + 4) % 4 * 2 + (at_z + dz) % 2

    ahead = (layer(0, 0, 1, 0), layer(0, 0, 0, 1))
    behind = (layer(0, 0, -1, 0), layer(0, 0, 0, -1))
    opposite = layer(0, 1, 0, 0)

    barrier = pltpu.get_barrier_semaphore()
    for other in ahead + behind + (opposite,):
        pl.semaphore_signal(
            barrier, inc=1, device_id={"depth": other}, device_id_type=MESH
        )
    for k in range(1, SLABS):
        pl.semaphore_signal(
            barrier, inc=1, device_id={"kslab": (slab + k) % SLABS}, device_id_type=MESH
        )
    for c in range(CHUNKS):
        for h in range(2):
            own_copy(c, h).start()

    pl.semaphore_wait(barrier, 5 + SLABS - 1)

    def send(c, h, offset, axis, step, half=None):
        dz, da, db = offset
        if axis == "z":
            there, to = slot(dz + 1, da, db), opposite
        else:
            at = h if axis == "a" else 1 - h
            to = ahead[at] if step > 0 else behind[at]
            there = slot(dz, da - step, db) if axis == "a" else slot(dz, da, db - step)
        source, target = held[c].at[h, slot(*offset)], held[c].at[h, there]
        if half is not None:
            source, target = held[c].at[h, slot(*offset), half], held[c].at[h, there, half]
        pltpu.make_async_remote_copy(
            src_ref=source, dst_ref=target,
            send_sem=send_sem.at[c, h], recv_sem=recv_sem.at[c, h, there],
            device_id={"depth": to}, device_id_type=MESH,
        ).start()

    def arrived(c, h, *offset):
        ref = held[c].at[h, slot(*offset)]
        pltpu.make_async_remote_copy(
            src_ref=ref, dst_ref=ref,
            send_sem=send_sem.at[c, h], recv_sem=recv_sem.at[c, h, slot(*offset)],
            device_id={"depth": opposite}, device_id_type=MESH,
        ).wait_recv()

    def along(c, h, axis, *offset):
        send(c, h, offset, axis, 1)
        send(c, h, offset, axis, -1)

    def own(c):
        for h in range(2):
            own_copy(c, h).wait()
            send(c, h, (0, 0, 0), "z", 1)
            along(c, h, "a", 0, 0, 0)
        for h in range(2):
            along(c, h, "b", 0, 0, 0)

    def partner(c):
        for h in range(2):
            arrived(c, h, 1, 0, 0)
            if CROSSINGS[c] == 1:
                along(c, h, "a", 1, 0, 0)
            if CROSSINGS[c] < 6:
                along(c, h, "b", 1, 0, 0)

    def near(c, dz):
        in_plane = dz == 0 or CROSSINGS[c] == 1
        for h in range(2):
            arrived(c, h, dz, -1, 0)
            if in_plane:
                send(c, h, (dz, -1, 0), "a", 1, 0)
            arrived(c, h, dz, 1, 0)
            if in_plane:
                send(c, h, (dz, 1, 0), "a", -1, 1)
            if dz == 0 and CROSSINGS[c] > 1:
                send(c, h, (0, -1, 0), "z", 1)
                send(c, h, (0, 1, 0), "z", 1)
            along(c, h, "b", dz, -1, 0)
            along(c, h, "b", dz, 1, 0)

    def far(c, dz):
        for h in range(2):
            arrived(c, h, dz, 2, 0)
            if dz == 0 and CROSSINGS[c] > 1:
                send(c, h, (0, 2, 0), "z", 1)
            along(c, h, "b", dz, 2, 0)

    def relay(c, dz, da):
        for h in range(2):
            arrived(c, h, dz, da, -1)
            send(c, h, (dz, da, -1), "b", 1, 0)
            arrived(c, h, dz, da, 1)
            send(c, h, (dz, da, 1), "b", -1, 1)
            if dz == 0 and da == 0 and CROSSINGS[c] == 6:
                send(c, h, (0, 0, -1), "z", 1)
                send(c, h, (0, 0, 1), "z", 1)

    def last(c, dz):
        for h in range(2):
            for da in range(4):
                arrived(c, h, dz, da, 2)

    def contract(c, offsets, start=False, end=False, parts=(0, 1)):
        for h in parts:
            row, low, col = corner(c, h)
            layers = [layer(h, *offset) for offset in offsets]
            slots = [slot(*offset) for offset in offsets]

            def column(j, carry, h=h, row=row, low=low, col=col, layers=layers, slots=slots):
                cs = pl.ds(pl.multiple_of(j * WIDE, WIDE), WIDE)
                wide = pl.ds(pl.multiple_of(col + j * WIDE, WIDE), WIDE)
                here = pl.ds(low, TILE)
                re = None if start else partial[0, here, wide]
                im = None if start else partial[1, here, wide]
                for s, k in zip(layers, slots):
                    gr = coeffs[s, 0, pl.ds(row, TILE), wide].astype(jnp.float32)
                    gi = coeffs[s, 1, pl.ds(row, TILE), wide].astype(jnp.float32)
                    xr = held[c][h, k, 0, :, cs].astype(jnp.float32)
                    xi = held[c][h, k, 1, :, cs].astype(jnp.float32)
                    more_re = gr * xr - gi * xi
                    more_im = gr * xi + gi * xr
                    re = more_re if re is None else re + more_re
                    im = more_im if im is None else im + more_im
                if end:
                    summed[here, wide] = re.astype(jnp.bfloat16)
                    summed[pl.ds(SIZES[c] + low, TILE), wide] = im.astype(jnp.bfloat16)
                else:
                    partial[0, here, wide] = re
                    partial[1, here, wide] = im
                return carry
            lax.fori_loop(0, width(c) // WIDE, column, 0)

    def finish(c):
        for at, pair in enumerate(LAST):
            for h in range(2):
                for da in pair:
                    arrived(c, h, 1, da, 2)
                offsets = [(1, da, 2) for da in pair]
                contract(c, offsets, end=at == len(LAST) - 1, parts=(h,))

    def peer(k):
        chip = (slab // 2 + (2, 3, 1, 0)[k // 2]) % 4
        return chip * 2 + (slab + 1 + k) % 2

    peers = [peer(k) for k in range(SLABS)]

    def swap(c, k):
        return pltpu.make_async_remote_copy(
            src_ref=outgoing[c].at[k], dst_ref=halves[c].at[slab],
            send_sem=swap_send.at[c, k], recv_sem=swap_recv.at[c, slab],
            device_id={"kslab": peers[k]}, device_id_type=MESH,
        )

    def transform_y(c):
        n = SIZES[c]
        for group in GROUPS:
            results = []
            for k in group:
                both = jnp.dot(summed[:2 * n], ty[peers[k]], preferred_element_type=jnp.float32)
                re = both[:n, :COLS] - both[n:, COLS:]
                im = both[:n, COLS:] + both[n:, :COLS]
                results.append(jnp.concatenate([re, im], axis=1).astype(jnp.bfloat16))
            for k, result in zip(group, results):
                if k < SLABS - 1:
                    outgoing[c][k] = result
                else:
                    halves[c][slab] = result
            for k in group:
                if k < SLABS - 1:
                    swap(c, k).start()

    def swapped(c):
        for k in reversed(range(SLABS - 1)):
            pltpu.make_async_remote_copy(
                src_ref=outgoing[c].at[k], dst_ref=halves[c].at[peers[k]],
                send_sem=swap_send.at[c, k], recv_sem=swap_recv.at[c, peers[k]],
                device_id={"kslab": peers[k]}, device_id_type=MESH,
            ).wait_recv()

    def by_table(c, rows):
        columns = pl.ds(STARTS[c] * SLABS, SIZES[c] * SLABS)
        incoming = halves[c][...].reshape(SLABS * SIZES[c], 2 * COLS)
        return jnp.dot(tx[rows, columns], incoming, preferred_element_type=jnp.float32)

    def gather_x(c):
        for i in range(8):
            rows = pl.ds(i * 128, 128)
            term = by_table(c, rows)
            gathered[rows] = term if c == 0 else gathered[rows] + term

    loads = [
        pltpu.make_async_copy(green.at[0], coeffs, load_sem.at[0]),
        pltpu.make_async_copy(table_y, ty, load_sem.at[1]),
        pltpu.make_async_copy(table_x, tx, load_sem.at[2]),
        pltpu.make_async_copy(contrast.at[0], con, load_sem.at[3]),
    ]

    def start_loads():
        for load in loads:
            load.start()

    def wait_loads():
        for load in loads:
            load.wait()

    early0 = [(0, da, db) for da in (0, 1, -1, 2) for db in (0, 1, -1)]
    early1 = [(1, da, db) for da in (0, 1, -1, 2) for db in (0, 1, -1)]
    late0 = [(0, da, 2) for da in range(4)]
    late1 = [(1, da, 2) for da in range(4)]

    own(1)
    start_loads()
    own(0)
    near(1, 0)
    partner(1)
    near(0, 0)
    near(1, 1)
    far(0, 0)
    partner(0)
    relay(0, 0, 1)
    relay(0, 0, 0)
    relay(0, 0, -1)
    near(0, 1)
    relay(0, 0, 2)
    far(1, 0)
    relay(0, 1, 1)
    far(0, 1)
    wait_loads()
    contract(0, early0, start=True)
    relay(1, 0, 0)
    relay(0, 1, 0)
    relay(0, 1, -1)
    relay(0, 1, 2)
    relay(1, 0, 2)
    far(1, 1)
    contract(0, early1)
    relay(1, 0, -1)
    last(0, 0)
    contract(0, late0)
    relay(1, 0, 1)
    relay(1, 1, -1)
    last(0, 1)
    contract(0, late1, end=True)
    relay(1, 1, 1)
    transform_y(0)
    relay(1, 1, 2)
    relay(1, 1, 0)
    last(1, 0)
    contract(1, early0, start=True)
    contract(1, early1)
    contract(1, late0)
    finish(1)
    transform_y(1)

    for c in range(CHUNKS - 1):
        swapped(c)
        gather_x(c)
    for c in range(CHUNKS):
        for h in range(2):
            sent = held[c].at[h, pl.ds(0, LAYERS - 1)]
            pltpu.make_async_remote_copy(
                src_ref=sent, dst_ref=sent,
                send_sem=send_sem.at[c, h], recv_sem=recv_sem.at[c, h, 0],
                device_id={"depth": opposite}, device_id_type=MESH,
            ).wait_send()
        for k in range(SLABS - 1):
            swap(c, k).wait_send()
    swapped(CHUNKS - 1)
    for i in range(4):
        rows = pl.ds(i * 128, 128)
        low = pl.ds(NX + i * 128, 128)
        by_cos = gathered[rows] + by_table(CHUNKS - 1, rows)
        by_sin = gathered[low] + by_table(CHUNKS - 1, low)
        scale = con[rows]
        out[0, 0, rows] = ((by_cos[:, :COLS] - by_sin[:, COLS:]) * scale).astype(jnp.bfloat16)
        out[0, 1, rows] = ((by_sin[:, :COLS] + by_cos[:, COLS:]) * scale).astype(jnp.bfloat16)


def on_device(spectra, green, contrast):
    cos_y, sin_y = fourier_tables(NY)
    table_y = np.stack(
        [
            np.concatenate(
                [cos_y[:, j * COLS:(j + 1) * COLS], sin_y[:, j * COLS:(j + 1) * COLS]], axis=1
            )
            for j in range(SLABS)
        ]
    )
    cos_x, sin_x = fourier_tables(NX)
    order = np.concatenate(
        [
            (np.arange(SLABS)[:, None] * ROWS + STARTS[c] + np.arange(SIZES[c])[None]).reshape(-1)
            for c in range(CHUNKS)
        ]
    )
    table_x = np.concatenate([cos_x, sin_x], axis=0)[:, order]
    operands = [
        pltpu.with_memory_space_constraint(operand, pltpu.MemorySpace.HBM)
        for operand in (spectra, green, contrast, jnp.asarray(table_y), jnp.asarray(table_x))
    ]
    return pl.pallas_call(
        kernel,
        out_shape=jax.ShapeDtypeStruct((1, 2, NX, COLS), jnp.bfloat16),
        in_specs=[pl.BlockSpec(memory_space=pl.ANY)] * 5,
        out_specs=pl.BlockSpec(memory_space=pltpu.VMEM),
        scratch_shapes=[
            pltpu.VMEM((LAYERS, 2, ROWS, NY), jnp.bfloat16),
            pltpu.VMEM((SLABS, NY, 2 * COLS), jnp.bfloat16),
            pltpu.VMEM((2 * NX, NX), jnp.bfloat16),
            pltpu.VMEM((NX, COLS), jnp.float32),
            pltpu.VMEM((2, 2 * TILE, NY), jnp.float32),
            pltpu.VMEM((4 * TILE, NY), jnp.bfloat16),
            pltpu.VMEM((2 * NX, 2 * COLS), jnp.float32),
            pltpu.SemaphoreType.DMA((CHUNKS, 2)),
            pltpu.SemaphoreType.DMA((4,)),
            pltpu.SemaphoreType.DMA((CHUNKS, 2)),
            pltpu.SemaphoreType.DMA((CHUNKS, 2, LAYERS)),
            pltpu.SemaphoreType.DMA((CHUNKS, SLABS)),
            pltpu.SemaphoreType.DMA((CHUNKS, SLABS)),
        ]
        + [pltpu.VMEM((2, LAYERS, 2, TILE, width(c)), jnp.bfloat16) for c in range(CHUNKS)]
        + [pltpu.VMEM((SLABS, SIZES[c], 2 * COLS), jnp.bfloat16) for c in range(CHUNKS)] * 2,
        compiler_params=pltpu.CompilerParams(
            collective_id=0, has_side_effects=True, vmem_limit_bytes=44 * 1024 * 1024
        ),
    )(*operands)


def solution(mesh):
    in_specs = (
        P("depth", None, "kslab", None),
        P("depth", None, None, "kslab", None),
        P("depth", None, "kslab"),
    )
    out_specs = P("depth", None, None, "kslab")
    return jax.shard_map(
        on_device, mesh=mesh, in_specs=in_specs, out_specs=out_specs, check_vma=False
    )
```
